32 devices in a mesh: grp: 2 (over x), wide: 16 (over z, y, core).
Axes of the slice: x: 2, y: 2, z: 4, core: 2. Of those that a mesh axis runs over, the one named last changes fastest.
Arguments:
- queries: bfloat16 [256, 4096], P(('grp', 'wide')), parts along dimension 0, may hold values from -8 to 8
- draft_keys: bfloat16 [256, 512], P(('grp', 'wide')), parts along dimension 0, may hold values from -8 to 8
- draft_values: bfloat16 [256, 512], P(('grp', 'wide')), parts along dimension 0, may hold values from -24 to 24
- cache_keys: bfloat16 [262144, 128], P(('grp', 'wide')), parts along dimension 0, may hold values from -8 to 8
- cache_values: bfloat16 [262144, 128], P(('grp', 'wide')), parts along dimension 0, may hold values from -24 to 24
- block_owner: int32 [32], P('grp'), parts along dimension 0, may hold values from 0 to 15, each once
- block_lengths: int32 [32], P('grp'), parts along dimension 0, may hold values from 1024 to 8192, as said below
- draft_mask: int32 [4, 64, 64], P('grp'), parts along dimension 0, may hold values from 0 to 1, as said below
- out_weight: bfloat16 [4096, 8192], P(None, 'wide'), may hold values from -1 to 1
- norm_gain: float32 [8192], replicated, may hold values from 0.25 to 1.75
- gate_weight: bfloat16 [8192, 14336], P(None, 'wide'), may hold values from -0.0625 to 0.0625
- up_weight: bfloat16 [8192, 14336], P(None, 'wide'), may hold values from -0.0625 to 0.0625
Outputs:
- projected: bfloat16 [256, 8192], P('grp', 'wide'), parts along dimension 0
- hidden: bfloat16 [256, 14336], P('grp', 'wide'), parts along dimension 0
The draws below stay inside these ranges and needn't reach their ends.
There are 2 independent parts, one for each index of `grp`. The reference program is written for one: setup_inputs(seed, part) draws one part's arguments, and reference() takes and returns one part's arrays. A program takes and returns all parts, laid end to end along the dimension named above; an argument that names none is the same for every part. Nothing has to cross between parts.
Inputs may be any that keep to these rules, and one draw needn't show every extreme that they name: `block_owner`: each device holds exactly one block. `block_lengths`: at most 8192 rows a block, and some block has exactly 8192 rows. In each sequence row 0 is the root of a tree in which every other row's parent lies 1 to 4 rows before it; draft_mask[s, i, t] is 1 exactly when t is i or an ancestor of i.
All inputs are finite; a program needn't handle non-finite values.
Results may differ from the reference program's by a relative error of at most 0.02.
Values may be sent and summed in bfloat16 or wider, within the bound.
A program may use at most 128 MiB of HBM per device.

```python
import math
import jax
import jax.numpy as jnp
from jax import lax

D = 8192
KVH = 4
GROUP = 8
HD = 128
FF = 14336
SEQS = 2
DRAFT = 64
CAP = 8192
ROWS = 128
N_WIDE = 16


def draw_queries(key, part):
    own = jax.random.fold_in(key, 101)
    shape = (ROWS, KVH * GROUP * HD)
    base = jnp.clip(2.0 * jax.random.normal(own, shape, jnp.float32), -8.0, 8.0)
    return base.astype(jnp.bfloat16)


def draw_cache_keys(key, part):
    own = jax.random.fold_in(key, 202)
    shape = (N_WIDE * CAP, HD)
    base = jnp.clip(jax.random.normal(own, shape, jnp.float32), -8.0, 8.0)
    return base.astype(jnp.bfloat16)


def draw_block_lengths(key, part):
    first, second, third = jax.random.split(jax.random.fold_in(key, 303), 3)
    left = jax.random.randint(first, (N_WIDE,), 0, CAP, jnp.int32)
    right = jax.random.randint(second, (N_WIDE,), 0, CAP, jnp.int32)
    lengths = CAP // 8 + left * right // CAP * 7 // 8
    chosen = jax.random.randint(third, (), 0, N_WIDE, jnp.int32)
    return jnp.where(jnp.arange(N_WIDE, dtype=jnp.int32) == chosen, CAP, lengths).astype(jnp.int32)


def draw_draft_mask(key, part):
    steps_back = jax.random.randint(jax.random.fold_in(key, 404), (SEQS, DRAFT), 1, 5, jnp.int32)
    index = jnp.arange(DRAFT, dtype=jnp.int32)
    parent = jnp.maximum(index[None, :] - steps_back, 0)
    link = (index[None, None, :] == parent[:, :, None]) & (index[None, :, None] > 0)
    reach = link.astype(jnp.int32) + jnp.eye(DRAFT, dtype=jnp.int32)[None]
    levels = int(math.log2(DRAFT)) + 1
    for repeat in range(levels):
        reach = jnp.minimum(jnp.matmul(reach, reach), 1)
    return reach.astype(jnp.int32)


def draw_out_weight(key, part):
    first, second = jax.random.split(jax.random.fold_in(key, 505))
    fan_width = KVH * GROUP * HD
    entries = jax.random.normal(first, (fan_width, D), jnp.float32) / math.sqrt(fan_width)
    spread = jnp.exp(jax.random.uniform(second, (D,), jnp.float32, 0.0, math.log(10.0)))
    position = jnp.arange(D, dtype=jnp.float32) / D
    ramp = jnp.exp(position * math.log(3.0))
    return jnp.clip(entries * (spread * ramp / 8.0)[None, :], -1.0, 1.0).astype(jnp.bfloat16)


def block_scale(key, dims, cuts, smallest, largest):
    def one(dim, parts):
        draws = jax.random.uniform(jax.random.fold_in(jax.random.fold_in(key, 6), dim), (parts,), jnp.float32, smallest / len(cuts), largest / len(cuts))
        return jnp.repeat(jnp.exp(draws), dims[dim] // parts).reshape((-1,) + (1,) * (len(dims) - dim - 1))

    loudness = one(*cuts[0])
    for cut in cuts[1:]:
        loudness = loudness * one(*cut)
    return loudness


def noise(rng, extent, deviation, most, cuts=(), held_as=jnp.bfloat16):
    gain = block_scale(rng, extent, cuts, -0.22, 0.18) if cuts else 1.0
    result = jax.random.normal(rng, extent, jnp.float32) * deviation * gain
    return jnp.minimum(jnp.maximum(result, -most), most).astype(held_as)


def setup_inputs(seed: int = 0, part: int = 0) -> dict:
    key_of = jax.random.split(jax.random.key(seed), 13)
    part_splits = jax.random.split(jax.random.fold_in(key_of[12], part), 13)
    return {
        "queries": draw_queries(jax.random.fold_in(jax.random.fold_in(key_of[12], part), 71), part),
        "draft_keys": noise(part_splits[1], (ROWS, KVH * HD), 2.0, 8.0, ((0, 16),)),
        "draft_values": noise(part_splits[2], (ROWS, KVH * HD), 4.0, 24.0, ((0, 16),)),
        "cache_keys": draw_cache_keys(jax.random.fold_in(jax.random.fold_in(key_of[12], part), 71), part),
        "cache_values": noise(part_splits[4], (N_WIDE * CAP, HD), 4.0, 24.0, ((0, 16),)),
        "block_owner": jax.random.permutation(part_splits[5], N_WIDE).astype(jnp.int32),
        "block_lengths": draw_block_lengths(jax.random.fold_in(jax.random.fold_in(key_of[12], part), 71), part),
        "draft_mask": draw_draft_mask(jax.random.fold_in(jax.random.fold_in(key_of[12], part), 71), part),
        "out_weight": draw_out_weight(jax.random.fold_in(key_of[12], 71), part),
        "norm_gain": jnp.clip(1.0 + 0.15 * jax.random.normal(key_of[9], (D,), jnp.float32), 0.25, 1.75),
        "gate_weight": noise(key_of[10], (D, FF), D ** -0.5, 0.0625, ((1, 16),)),
        "up_weight": noise(key_of[11], (D, FF), D ** -0.5, 0.0625, ((1, 16),)),
    }


very_low = -1e+30
epsilon = 1e-05

def block_update(state, query_rows, block_keys, block_values, valid, scale):
    running, total, weighted = state
    scores = jnp.einsum('igc,kc->igk', query_rows.astype(jnp.float32), block_keys.astype(jnp.float32), precision=lax.Precision.HIGHEST) * scale
    scores = jnp.where(valid, scores, very_low)
    newest = jnp.maximum(running, lax.optimization_barrier(jnp.max(scores, axis=-1)))
    factor = jnp.exp(running - newest)
    weights = jnp.where(valid, jnp.exp(scores - newest[..., None]), 0.0)
    total = total * factor + lax.optimization_barrier(jnp.sum(weights, axis=-1))
    rounded = lax.optimization_barrier(weights.astype(jnp.bfloat16))
    weighted = weighted * factor[..., None] + jnp.einsum('igk,kc->igc', rounded.astype(jnp.float32), block_values.astype(jnp.float32), precision=lax.Precision.HIGHEST)
    return (newest, total, weighted)

def attend(query_rows, keys, values, length, own_keys, own_values, own_valid):
    block_size = min(512, keys.shape[0])
    scale = 1.0 / math.sqrt(query_rows.shape[2])
    rows_count = query_rows.shape[0]
    heads = query_rows.shape[1]
    state = (jnp.full((rows_count, heads), very_low, jnp.float32), jnp.zeros((rows_count, heads), jnp.float32), jnp.zeros((rows_count, heads, query_rows.shape[2]), jnp.float32))
    offsets = jnp.arange(block_size, dtype=jnp.int32)

    def advance(number, carry):
        begin = (number * block_size).astype(jnp.int32)
        block_keys = lax.dynamic_slice_in_dim(keys, begin, block_size, 0)
        block_values = lax.dynamic_slice_in_dim(values, begin, block_size, 0)
        valid = (begin + offsets < length)[None, None, :]
        return block_update(carry, query_rows, block_keys, block_values, valid, scale)
    count = ((length + block_size - 1) // block_size).astype(jnp.int32)
    state = lax.fori_loop(jnp.int32(0), count, advance, state)
    return block_update(state, query_rows, own_keys, own_values, own_valid[:, None, :], scale)

def reference(queries, draft_keys, draft_values, cache_keys, cache_values, block_owner, block_lengths, draft_mask, out_weight, norm_gain, gate_weight, up_weight):
    blocks_per_pair = N_WIDE // (SEQS * KVH)
    group_width = GROUP * HD

    def one_pair(pair):
        sequence = pair // KVH
        head = pair % KVH
        row_start = (sequence * DRAFT).astype(jnp.int32)
        rows = lax.dynamic_slice_in_dim(lax.dynamic_slice_in_dim(queries, row_start, DRAFT, 0), (head * group_width).astype(jnp.int32), group_width, 1).reshape(DRAFT, GROUP, HD)
        own_keys = lax.dynamic_slice_in_dim(lax.dynamic_slice_in_dim(draft_keys, row_start, DRAFT, 0), (head * HD).astype(jnp.int32), HD, 1)
        own_values = lax.dynamic_slice_in_dim(lax.dynamic_slice_in_dim(draft_values, row_start, DRAFT, 0), (head * HD).astype(jnp.int32), HD, 1)
        visible = lax.dynamic_index_in_dim(draft_mask, sequence, 0, keepdims=False) > 0

        def one_block(position):
            index = (pair * blocks_per_pair + position).astype(jnp.int32)
            owner = lax.dynamic_index_in_dim(block_owner, index, 0, keepdims=False)
            length = lax.dynamic_index_in_dim(block_lengths, index, 0, keepdims=False)
            keys = lax.dynamic_slice_in_dim(cache_keys, (owner * CAP).astype(jnp.int32), CAP, 0)
            values = lax.dynamic_slice_in_dim(cache_values, (owner * CAP).astype(jnp.int32), CAP, 0)
            valid = visible & (position == blocks_per_pair - 1)
            peak, total, weighted = attend(rows, keys, values, length, own_keys, own_values, valid)
            output = lax.optimization_barrier((weighted / total[..., None]).astype(jnp.bfloat16)).astype(jnp.float32)
            return (peak, total, output)
        maxima, totals, outputs = lax.map(one_block, jnp.arange(blocks_per_pair, dtype=jnp.int32))
        highest = lax.optimization_barrier(jnp.max(maxima, axis=0))
        mixing = jnp.exp(maxima - highest[None]) * totals
        total = lax.optimization_barrier(jnp.sum(mixing, axis=0))
        weighted = lax.optimization_barrier(jnp.sum(mixing[..., None] * outputs, axis=0))
        return (weighted / total[..., None]).astype(jnp.bfloat16)
    pairs = lax.map(one_pair, jnp.arange(SEQS * KVH, dtype=jnp.int32))
    attended = pairs.reshape(SEQS, KVH, DRAFT, GROUP * HD).transpose(0, 2, 1, 3).reshape(SEQS * DRAFT, KVH * GROUP * HD)
    projected = jnp.dot(attended, out_weight, preferred_element_type=jnp.float32).astype(jnp.bfloat16)
    branch = lax.optimization_barrier(projected).astype(jnp.float32)
    inverse = lax.rsqrt(lax.optimization_barrier(jnp.sum(branch * branch, axis=1)) / D + epsilon)
    normed = (branch * inverse[:, None] * norm_gain[None, :]).astype(jnp.bfloat16)
    gate = jnp.dot(normed, gate_weight, preferred_element_type=jnp.float32)
    upward = jnp.dot(normed, up_weight, preferred_element_type=jnp.float32)
    hidden = (jax.nn.silu(gate) * upward).astype(jnp.bfloat16)
    return (projected, hidden)
```

```python
import functools
import math

import jax
import jax.numpy as jnp
from jax import lax
from jax.experimental import pallas as pl
from jax.experimental.pallas import tpu as pltpu
from jax.sharding import PartitionSpec as P

very_low = -1e30
epsilon = 1e-05
tiles = 4
chunk_rows = 1024
weight_parts = 4


def block_update(state, query_rows, block_keys, block_values, valid, scale):
    running, total, weighted = state
    scores = (
        jnp.einsum("igc,kc->igk", query_rows, block_keys, preferred_element_type=jnp.float32)
        * scale
    )
    scores = jnp.where(valid, scores, very_low)
    newest = jnp.maximum(running, jnp.max(scores, axis=-1))
    factor = jnp.exp(running - newest)
    weights = jnp.where(valid, jnp.exp(scores - newest[..., None]), 0.0)
    total = total * factor + jnp.sum(weights, axis=-1)
    weighted = weighted * factor[..., None] + jnp.einsum(
        "igk,kc->igc",
        weights.astype(jnp.bfloat16),
        block_values,
        preferred_element_type=jnp.float32,
    )
    return (newest, total, weighted)


def attend(query_rows, keys, values, length, own_keys, own_values, own_valid):
    block_size = min(512, keys.shape[0])
    scale = 1.0 / math.sqrt(query_rows.shape[2])
    rows_count = query_rows.shape[0]
    heads = query_rows.shape[1]
    state = (
        jnp.full((rows_count, heads), very_low, jnp.float32),
        jnp.zeros((rows_count, heads), jnp.float32),
        jnp.zeros((rows_count, heads, query_rows.shape[2]), jnp.float32),
    )
    offsets = jnp.arange(block_size, dtype=jnp.int32)

    def advance(number, carry):
        begin = (number * block_size).astype(jnp.int32)
        block_keys = lax.dynamic_slice_in_dim(keys, begin, block_size, 0)
        block_values = lax.dynamic_slice_in_dim(values, begin, block_size, 0)
        valid = (begin + offsets < length)[None, None, :]
        return block_update(carry, query_rows, block_keys, block_values, valid, scale)

    count = (length + block_size - 1) // block_size
    state = lax.fori_loop(jnp.int32(0), count, advance, state)
    return block_update(state, query_rows, own_keys, own_values, own_valid[:, None, :], scale)


def plain_device(
    queries,
    draft_keys,
    draft_values,
    cache_keys,
    cache_values,
    block_owner,
    block_lengths,
    draft_mask,
    out_weight,
    norm_gain,
    gate_weight,
    up_weight,
):
    devices = lax.axis_size("wide")
    own_index = lax.axis_index("wide")
    head_size = cache_keys.shape[1]
    key_heads = draft_keys.shape[1] // head_size
    group_width = queries.shape[1] // key_heads
    group = group_width // head_size
    sequences = draft_mask.shape[0]
    draft_rows = draft_mask.shape[1]
    all_rows = sequences * draft_rows
    local_rows = queries.shape[0]
    heads_all = key_heads * group
    blocks_per_pair = devices // (sequences * key_heads)
    device_ids = jnp.arange(devices, dtype=jnp.int32)
    owned = (block_owner[None, :] == device_ids[:, None]).astype(jnp.int32)
    device_block = jnp.sum(owned * device_ids[None, :], axis=1)
    device_pair = device_block // blocks_per_pair
    device_sequence = device_pair // key_heads
    device_head = device_pair % key_heads
    device_length = jnp.sum(owned * block_lengths[None, :], axis=1)
    picker = (device_ids == own_index).astype(jnp.int32)
    own_block = jnp.sum(picker * device_block)
    own_sequence = jnp.sum(picker * device_sequence)
    own_head = jnp.sum(picker * device_head)
    own_length = jnp.sum(picker * device_length)
    is_last = own_block % blocks_per_pair == blocks_per_pair - 1
    row_start = own_sequence * draft_rows
    head_numbers = jnp.arange(key_heads, dtype=jnp.int32)
    every_query, every_key, every_value = (
        lax.all_gather(queries, "wide", axis=0, tiled=True),
        lax.all_gather(draft_keys, "wide", axis=0, tiled=True),
        lax.all_gather(draft_values, "wide", axis=0, tiled=True),
    )
    query_columns = own_head * group_width
    key_columns = own_head * head_size
    pair_queries = lax.dynamic_slice_in_dim(
        lax.dynamic_slice_in_dim(every_query, row_start, draft_rows, 0),
        query_columns,
        group_width,
        1,
    )
    pair_keys = lax.dynamic_slice_in_dim(
        lax.dynamic_slice_in_dim(every_key, row_start, draft_rows, 0), key_columns, head_size, 1
    )
    pair_values = lax.dynamic_slice_in_dim(
        lax.dynamic_slice_in_dim(every_value, row_start, draft_rows, 0), key_columns, head_size, 1
    )
    own_head = jnp.sum(picker * device_head)
    query_rows = pair_queries.reshape(draft_rows, group, head_size)
    own_valid = (
        lax.dynamic_index_in_dim(draft_mask, own_sequence, 0, keepdims=False) > 0
    ) & is_last
    running, total, weighted = attend(
        query_rows, cache_keys, cache_values, own_length, pair_keys, pair_values, own_valid
    )
    block_output = (weighted / total[..., None]).astype(jnp.bfloat16)
    slot_peak = lax.dynamic_update_slice(
        jnp.full((all_rows, group), very_low, jnp.float32), running, (row_start, jnp.int32(0))
    ).reshape(devices, local_rows, group)
    slot_total = lax.dynamic_update_slice(
        jnp.zeros((all_rows, group), jnp.float32), total, (row_start, jnp.int32(0))
    ).reshape(devices, local_rows, group)
    slot_output = lax.dynamic_update_slice(
        jnp.zeros((all_rows, group, head_size), jnp.bfloat16),
        block_output,
        (row_start, jnp.int32(0), jnp.int32(0)),
    ).reshape(devices, local_rows, group, head_size)
    back_peak, back_total = (
        lax.all_to_all(slot_peak, "wide", split_axis=0, concat_axis=0, tiled=True),
        lax.all_to_all(slot_total, "wide", split_axis=0, concat_axis=0, tiled=True),
    )
    back_output = lax.all_to_all(slot_output, "wide", split_axis=0, concat_axis=0, tiled=True)
    member = device_head[:, None] == head_numbers[None, :]
    spread = jnp.where(member[:, None, :, None], back_peak[:, :, None, :], very_low)
    highest = jnp.max(spread, axis=0)
    mixing = jnp.exp(spread - highest[None]) * back_total[:, :, None, :]
    row_total = jnp.sum(mixing, axis=0)
    row_weighted = jnp.einsum(
        "srgj,srjc->rgjc", mixing, back_output.astype(jnp.float32), precision=lax.Precision.HIGHEST
    )
    attended_rows = (
        (row_weighted / row_total[..., None])
        .astype(jnp.bfloat16)
        .reshape(local_rows, heads_all * head_size)
    )
    combined = jnp.dot(
        lax.all_gather(attended_rows, "wide", axis=0, tiled=True),
        out_weight,
        preferred_element_type=jnp.float32,
    )
    projected = combined.astype(jnp.bfloat16)
    columns = projected.shape[1]
    branch = lax.optimization_barrier(projected).astype(jnp.float32)
    squares = lax.psum(jnp.sum(branch * branch, axis=1), "wide")
    inverse = lax.rsqrt(squares / (columns * devices) + epsilon)
    gain_part = lax.dynamic_slice_in_dim(norm_gain, own_index * columns, columns, 0)
    normed = (branch * inverse[:, None] * gain_part[None, :]).astype(jnp.bfloat16)
    piece = lax.all_gather(normed, "wide", axis=1, tiled=True)
    gate = jnp.dot(piece, gate_weight, preferred_element_type=jnp.float32)
    upward = jnp.dot(piece, up_weight, preferred_element_type=jnp.float32)
    hidden = (jax.nn.silu(gate) * upward).astype(jnp.bfloat16)
    return (projected, hidden)


def fused_kernel(
    devices,
    owner_ref,
    lengths_ref,
    packed_ref,
    mask_ref,
    gain_ref,
    keys_hbm,
    values_hbm,
    out_hbm,
    gate_hbm,
    up_hbm,
    projected_ref,
    hidden_ref,
    sent,
    gathered,
    query_all,
    keys,
    values,
    outs,
    stats,
    attended,
    branch,
    gate_sum,
    up_sum,
    out_weight,
    gate_weight,
    up_weight,
    local_sem,
    direct_send,
    direct_recv,
    ring_send,
    ring_recv,
):
    me = lax.axis_index("wide")
    depth = devices // 4
    place_z, place_y, place_c = me // 4, lax.rem(me // 2, 2), lax.rem(me, 2)
    mirror_y = me + 2 - 4 * place_y
    mirror_c = me + 1 - 2 * place_c
    head_size = keys.shape[1]
    key_heads = packed_ref.shape[0]
    sequences, draft_rows = mask_ref.shape[0], mask_ref.shape[1]
    senders = devices // sequences
    local_rows = draft_rows // senders
    group = query_all.shape[0] // draft_rows
    blocks_per_pair = devices // (sequences * key_heads)
    capacity = keys.shape[0]

    def block_of(device):
        block = jnp.int32(0)
        for k in range(devices):
            block = block + jnp.where(owner_ref[k] == device, jnp.int32(k), jnp.int32(0))
        return jnp.minimum(block, devices - 1)

    key_copy = pltpu.make_async_copy(keys_hbm, keys, local_sem.at[0])
    value_copy = pltpu.make_async_copy(values_hbm, values, local_sem.at[1])
    key_copy.start()
    value_copy.start()

    barrier = pltpu.get_barrier_semaphore()

    def greet(k, carry):
        pl.semaphore_signal(
            barrier,
            inc=1,
            device_id={"wide": lax.rem(me + k, devices)},
            device_id_type=pl.DeviceIdType.MESH,
        )
        return carry

    lax.fori_loop(1, devices, greet, 0)

    def fill(k, carry):
        target = lax.rem(me + k, devices)
        head = lax.rem(block_of(target) // blocks_per_pair, key_heads)
        sent[target] = packed_ref[head]
        return carry

    lax.fori_loop(1, devices, fill, 0)
    own_block = block_of(me)
    own_pair = own_block // blocks_per_pair
    own_sequence = own_pair // key_heads
    own_head = lax.rem(own_pair, key_heads)
    is_last = jnp.where(
        lax.rem(own_block, blocks_per_pair) == blocks_per_pair - 1, jnp.int32(1), jnp.int32(0)
    )
    own_length = jnp.int32(0)
    for k in range(devices):
        own_length = own_length + jnp.where(owner_ref[k] == me, lengths_ref[k], jnp.int32(0))
    gathered[me] = packed_ref[own_head]
    pl.semaphore_wait(barrier, devices - 1)

    def direct(target, source):
        return pltpu.make_async_remote_copy(
            src_ref=sent.at[target],
            dst_ref=gathered.at[source],
            send_sem=direct_send.at[target],
            recv_sem=direct_recv.at[source],
            device_id={"wide": target},
            device_id_type=pl.DeviceIdType.MESH,
        )

    def send_direct(k, carry):
        direct(lax.rem(me + k, devices), me).start()
        return carry

    lax.fori_loop(1, devices, send_direct, 0)

    weight_copies = []
    for number, (source, target) in enumerate(
        ((out_hbm, out_weight), (gate_hbm, gate_weight), (up_hbm, up_weight))
    ):
        part = source.shape[0] // weight_parts
        for piece in range(weight_parts):
            rows = pl.ds(piece * part, part)
            weight_copies.append(
                pltpu.make_async_copy(
                    source.at[rows],
                    target.at[rows],
                    local_sem.at[2 + number * weight_parts + piece],
                )
            )
    for copy in weight_copies:
        copy.start()

    def wait_direct(k, carry):
        other = lax.rem(me + k, devices)
        descriptor = direct(other, other)
        descriptor.wait_send()
        descriptor.wait_recv()
        return carry

    lax.fori_loop(1, devices, wait_direct, 0)

    def hop(item, direction, source, target):
        buffer, phase = item
        return pltpu.make_async_remote_copy(
            src_ref=buffer.at[source],
            dst_ref=buffer.at[source],
            send_sem=ring_send.at[phase, direction, source],
            recv_sem=ring_recv.at[phase, source],
            device_id={"wide": target},
            device_id_type=pl.DeviceIdType.MESH,
        )

    def launch(items, upward, downward, source, begin):
        for item in items:
            for use, step, direction in ((upward, 4, 0), (downward, -4, 1)):
                if use:

                    @pl.when((place_z + step // 4 >= 0) & (place_z + step // 4 < depth))
                    def _(item=item, step=step, direction=direction):
                        copy = hop(item, direction, source, me + step)
                        copy.start() if begin else copy.wait_send()

            copy = hop(item, 2, source, mirror_y)
            copy.start() if begin else copy.wait_send()
            copy = hop(item, 3, source, mirror_c)
            copy.start() if begin else copy.wait_send()

    def own_send(items, begin=True):
        launch(items, True, True, me, begin)

    def z_step(items, distance, begin=True):
        @pl.when(place_z >= distance)
        def _():
            source = me - 4 * distance
            if begin:
                for item in items:
                    hop(item, 0, source, me).wait_recv()
            launch(items, True, False, source, begin)

        @pl.when(place_z + distance < depth)
        def _():
            source = me + 4 * distance
            if begin:
                for item in items:
                    hop(item, 1, source, me).wait_recv()
            launch(items, False, True, source, begin)

    def y_one(items, source, begin):
        for item in items:
            if begin:
                hop(item, 2, source, me).wait_recv()
            copy = hop(item, 3, source, mirror_c)
            copy.start() if begin else copy.wait_send()

    def y_step(items, distance, begin=True):
        if distance == 0:
            y_one(items, mirror_y, begin)
        else:

            @pl.when(place_z >= distance)
            def _():
                y_one(items, mirror_y - 4 * distance, begin)

            @pl.when(place_z + distance < depth)
            def _():
                y_one(items, mirror_y + 4 * distance, begin)

    def core_wait(items):
        for half in range(devices // 2):
            source = 2 * half + 1 - place_c
            for item in items:
                hop(item, 3, source, me).wait_recv()

    def finish_sends(items):
        own_send(items, False)
        for distance in range(1, depth):
            z_step(items, distance, False)
        for distance in range(depth):
            y_step(items, distance, False)

    pieces = [
        gathered[own_sequence * senders + number].astype(jnp.float32) for number in range(senders)
    ]

    def assembled(begin):
        return jnp.concatenate(
            [piece[begin : begin + local_rows] for piece in pieces], axis=0
        ).astype(jnp.bfloat16)

    for j in range(group):
        query_all[j * draft_rows : (j + 1) * draft_rows] = assembled(j * local_rows)
    draft_keys = assembled(group * local_rows)
    draft_values = assembled((group + 1) * local_rows)
    own_mask = mask_ref[own_sequence] * is_last

    tile_heads = group // tiles
    tile_rows = tile_heads * draft_rows
    unit = math.log2(math.e) / math.sqrt(head_size)
    steps = capacity // chunk_rows
    lanes = lax.broadcasted_iota(jnp.int32, (draft_rows, stats.shape[2]), 1)
    key_copy.wait()
    value_copy.wait()

    def update(state, scores, block_values):
        peak, total, weighted = state
        newest = jnp.maximum(peak, jnp.max(scores, axis=1, keepdims=True))
        factor = jnp.exp2(peak - newest)
        weights = jnp.exp2(scores - newest)
        total = total * factor + jnp.sum(weights, axis=1, keepdims=True)
        weighted = weighted * factor + jnp.dot(
            weights.astype(jnp.bfloat16), block_values, preferred_element_type=jnp.float32
        )
        return newest, total, weighted

    own_stats = jnp.zeros((draft_rows, stats.shape[2]), jnp.float32)
    for tile in range(tiles):
        query = query_all[tile * tile_rows : (tile + 1) * tile_rows]

        def advance(number, state, query=query):
            begin = pl.multiple_of(number * chunk_rows, chunk_rows)
            scores = lax.dot_general(
                query,
                keys[pl.ds(begin, chunk_rows)],
                (((1,), (1,)), ((), ())),
                preferred_element_type=jnp.float32,
            )
            position = begin + lax.broadcasted_iota(jnp.int32, (1, chunk_rows), 1)
            bias = jnp.where(position < own_length, 0.0, very_low)
            return update(state, scores * unit + bias, values[pl.ds(begin, chunk_rows)])

        state = (
            jnp.full((tile_rows, 1), very_low, jnp.float32),
            jnp.zeros((tile_rows, 1), jnp.float32),
            jnp.zeros((tile_rows, head_size), jnp.float32),
        )
        cuts = [steps * cut // depth for cut in range(depth + 1)]
        for cut in range(depth):
            state = lax.fori_loop(cuts[cut], cuts[cut + 1], advance, state)
            if tile > 0:
                before = [(outs.at[tile - 1], tile - 1)]
                if cut + 1 < depth:
                    z_step(before, cut + 1)
                else:
                    for distance in range(depth):
                        y_step(before, distance)
        scores = lax.dot_general(
            query, draft_keys, (((1,), (1,)), ((), ())), preferred_element_type=jnp.float32
        )
        visible = jnp.concatenate([own_mask] * tile_heads, axis=0) > 0
        peak, total, weighted = update(
            state, jnp.where(visible, scores * unit, very_low), draft_values
        )
        outs[tile, me] = (weighted / total).astype(jnp.bfloat16)
        for k in range(tile_heads):
            head = tile * tile_heads + k
            rows = slice(k * draft_rows, (k + 1) * draft_rows)
            own_stats = jnp.where(lanes == head, peak[rows], own_stats)
            own_stats = jnp.where(lanes == group + head, total[rows], own_stats)
        if tile + 1 == tiles:
            stats[me] = own_stats
            last = [(outs.at[tile], tile), (stats, tiles)]
            own_send(last)
        else:
            own_send([(outs.at[tile], tile)])

    for distance in range(1, depth):
        z_step(last, distance)
    for distance in range(depth):
        y_step(last, distance)
    core_wait([(outs.at[tile], tile) for tile in range(tiles)] + [(stats, tiles)])

    for pair in range(sequences * key_heads):
        owners = [owner_ref[pair * blocks_per_pair + b] for b in range(blocks_per_pair)]
        each = [stats[owner] for owner in owners]
        highest = functools.reduce(jnp.maximum, each)
        mixing = [
            jnp.exp2(one - highest) * pltpu.roll(one, one.shape[1] - group, 1) for one in each
        ]
        mixing_sum = functools.reduce(jnp.add, mixing)
        shares = [one / mixing_sum for one in mixing]
        top = pair // key_heads * draft_rows
        for tile in range(tiles):
            held = [outs[tile, owner].astype(jnp.float32) for owner in owners]
            for k in range(tile_heads):
                head = tile * tile_heads + k
                rows = slice(k * draft_rows, (k + 1) * draft_rows)
                mixed = functools.reduce(
                    jnp.add,
                    [share[:, head : head + 1] * one[rows] for share, one in zip(shares, held)],
                )
                left = (pair % key_heads * group + head) * head_size
                attended[top : top + draft_rows, left : left + head_size] = mixed.astype(
                    jnp.bfloat16
                )

    for copy in weight_copies[:weight_parts]:
        copy.wait()
    projected = jnp.dot(
        attended[...], out_weight[...], preferred_element_type=jnp.float32
    ).astype(jnp.bfloat16)
    branch[me] = projected
    phase = [(branch, tiles + 1)]
    own_send(phase)
    projected_ref[...] = projected
    for copy in weight_copies[weight_parts:]:
        copy.wait()

    columns = branch.shape[2]
    gate_sum[...] = jnp.zeros_like(gate_sum)
    up_sum[...] = jnp.zeros_like(up_sum)

    def absorb(source, squares):
        part = branch[source].astype(jnp.float32)
        scaled = (part * gain_ref[source]).astype(jnp.bfloat16)
        rows = pl.ds(pl.multiple_of(source * columns, columns), columns)
        gate_sum[...] += jnp.dot(scaled, gate_weight[rows], preferred_element_type=jnp.float32)
        up_sum[...] += jnp.dot(scaled, up_weight[rows], preferred_element_type=jnp.float32)
        return squares + jnp.sum(part * part, axis=1, keepdims=True)

    squares = absorb(me, jnp.zeros((branch.shape[1], 1), jnp.float32))
    z_step(phase, 1)
    y_step(phase, 0)
    squares = absorb(mirror_y, squares)
    for distance in range(2, depth):
        z_step(phase, distance)
        y_step(phase, distance - 1)
    y_step(phase, depth - 1)

    def absorb_plane(k, total):
        level = lax.rem(place_z + 1 + k // 2, depth)
        return absorb(4 * level + 2 * lax.rem(k, 2) + place_c, total)

    squares = lax.fori_loop(0, 2 * (depth - 1), absorb_plane, squares)

    def absorb_other(k, total):
        source = 2 * k + 1 - place_c
        hop(phase[0], 3, source, me).wait_recv()
        return absorb(source, total)

    squares = lax.fori_loop(0, devices // 2, absorb_other, squares)
    inverse = lax.rsqrt(squares / (columns * devices) + epsilon)
    gate = gate_sum[...] * inverse
    hidden_ref[...] = (gate / (1.0 + jnp.exp(-gate)) * (up_sum[...] * inverse)).astype(
        jnp.bfloat16
    )
    finish_sends([(outs.at[tile], tile) for tile in range(tiles)] + [(stats, tiles)] + phase)


def fused_device(
    queries,
    draft_keys,
    draft_values,
    cache_keys,
    cache_values,
    block_owner,
    block_lengths,
    draft_mask,
    out_weight,
    norm_gain,
    gate_weight,
    up_weight,
):
    devices = lax.axis_size("wide")
    capacity, head_size = cache_keys.shape
    key_heads = draft_keys.shape[1] // head_size
    group = queries.shape[1] // head_size // key_heads
    local_rows = queries.shape[0]
    sequences, draft_rows = draft_mask.shape[:2]
    rows = sequences * draft_rows
    columns, units = out_weight.shape[1], gate_weight.shape[1]

    def by_head(array, count):
        parted = array.reshape(local_rows, key_heads, count, head_size)
        return parted.transpose(1, 2, 0, 3).reshape(key_heads, count * local_rows, head_size)

    packed = jnp.concatenate(
        [by_head(queries, group), by_head(draft_keys, 1), by_head(draft_values, 1)], axis=1
    )
    vmem = pl.BlockSpec(memory_space=pltpu.VMEM)
    smem = pl.BlockSpec(memory_space=pltpu.SMEM)
    hbm = pl.BlockSpec(memory_space=pl.ANY)
    half = jnp.bfloat16
    return pl.pallas_call(
        functools.partial(fused_kernel, devices),
        out_shape=(
            jax.ShapeDtypeStruct((rows, columns), half),
            jax.ShapeDtypeStruct((rows, units), half),
        ),
        in_specs=[smem, smem, vmem, vmem, vmem, hbm, hbm, hbm, hbm, hbm],
        out_specs=(vmem, vmem),
        scratch_shapes=[
            pltpu.VMEM((devices,) + packed.shape[1:], half),
            pltpu.VMEM((devices,) + packed.shape[1:], half),
            pltpu.VMEM((group * draft_rows, head_size), half),
            pltpu.VMEM((capacity, head_size), half),
            pltpu.VMEM((capacity, head_size), half),
            pltpu.VMEM((tiles, devices, group // tiles * draft_rows, head_size), half),
            pltpu.VMEM((devices, draft_rows, head_size), jnp.float32),
            pltpu.VMEM((rows, out_weight.shape[0]), half),
            pltpu.VMEM((devices, rows, columns), half),
            pltpu.VMEM((rows, units), jnp.float32),
            pltpu.VMEM((rows, units), jnp.float32),
            pltpu.VMEM(out_weight.shape, half),
            pltpu.VMEM(gate_weight.shape, half),
            pltpu.VMEM(up_weight.shape, half),
            pltpu.SemaphoreType.DMA((2 + 3 * weight_parts,)),
            pltpu.SemaphoreType.DMA((devices,)),
            pltpu.SemaphoreType.DMA((devices,)),
            pltpu.SemaphoreType.DMA((tiles + 2, 4, devices)),
            pltpu.SemaphoreType.DMA((tiles + 2, devices)),
        ],
        compiler_params=pltpu.CompilerParams(
            collective_id=0, has_side_effects=True, vmem_limit_bytes=62 * 1024 * 1024
        ),
    )(
        block_owner,
        block_lengths,
        packed,
        draft_mask,
        norm_gain.reshape(devices, 1, columns),
        cache_keys,
        cache_values,
        out_weight,
        gate_weight,
        up_weight,
    )


def per_device(*arrays):
    queries, cache_keys, draft_mask = arrays[0], arrays[3], arrays[7]
    out_weight, gate_weight = arrays[8], arrays[10]
    head_size = cache_keys.shape[1]
    key_heads = arrays[1].shape[1] // head_size
    group = queries.shape[1] // head_size // key_heads
    whole_tiles = (
        queries.shape[0] % 8 == 0
        and lax.axis_size("wide") % 4 == 0
        and draft_mask.shape[1] % 8 == 0
        and head_size % 128 == 0
        and 2 * group <= head_size
        and group % tiles == 0
        and out_weight.shape[1] % 128 == 0
        and gate_weight.shape[1] % 128 == 0
        and cache_keys.shape[0] % chunk_rows == 0
        and out_weight.shape[0] % (16 * weight_parts) == 0
        and gate_weight.shape[0] % (16 * weight_parts) == 0
    )
    return fused_device(*arrays) if whole_tiles else plain_device(*arrays)


def solution(mesh):
    placed = (
        P(("grp", "wide"), None),
        P(("grp", "wide"), None),
        P(("grp", "wide"), None),
        P(("grp", "wide"), None),
        P(("grp", "wide"), None),
        P("grp"),
        P("grp"),
        P("grp", None, None),
        P(None, "wide"),
        P(),
        P(None, "wide"),
        P(None, "wide"),
    )
    return jax.shard_map(
        per_device,
        mesh=mesh,
        in_specs=placed,
        out_specs=(P("grp", "wide"), P("grp", "wide")),
        check_vma=False,
    )
```

```python
import functools
import math

import jax
import jax.numpy as jnp
from jax import lax
from jax.experimental import pallas as pl
from jax.experimental.pallas import tpu as pltpu
from jax.sharding import PartitionSpec as P

very_low = -1e30
epsilon = 1e-05
tiles = 2
chunk_rows = 1024
weight_parts = 4


def block_update(state, query_rows, block_keys, block_values, valid, scale):
    running, total, weighted = state
    scores = (
        jnp.einsum("igc,kc->igk", query_rows, block_keys, preferred_element_type=jnp.float32)
        * scale
    )
    scores = jnp.where(valid, scores, very_low)
    newest = jnp.maximum(running, jnp.max(scores, axis=-1))
    factor = jnp.exp(running - newest)
    weights = jnp.where(valid, jnp.exp(scores - newest[..., None]), 0.0)
    total = total * factor + jnp.sum(weights, axis=-1)
    weighted = weighted * factor[..., None] + jnp.einsum(
        "igk,kc->igc",
        weights.astype(jnp.bfloat16),
        block_values,
        preferred_element_type=jnp.float32,
    )
    return (newest, total, weighted)


def attend(query_rows, keys, values, length, own_keys, own_values, own_valid):
    block_size = min(512, keys.shape[0])
    scale = 1.0 / math.sqrt(query_rows.shape[2])
    rows_count = query_rows.shape[0]
    heads = query_rows.shape[1]
    state = (
        jnp.full((rows_count, heads), very_low, jnp.float32),
        jnp.zeros((rows_count, heads), jnp.float32),
        jnp.zeros((rows_count, heads, query_rows.shape[2]), jnp.float32),
    )
    offsets = jnp.arange(block_size, dtype=jnp.int32)

    def advance(number, carry):
        begin = (number * block_size).astype(jnp.int32)
        block_keys = lax.dynamic_slice_in_dim(keys, begin, block_size, 0)
        block_values = lax.dynamic_slice_in_dim(values, begin, block_size, 0)
        valid = (begin + offsets < length)[None, None, :]
        return block_update(carry, query_rows, block_keys, block_values, valid, scale)

    count = (length + block_size - 1) // block_size
    state = lax.fori_loop(jnp.int32(0), count, advance, state)
    return block_update(state, query_rows, own_keys, own_values, own_valid[:, None, :], scale)


def plain_device(
    queries,
    draft_keys,
    draft_values,
    cache_keys,
    cache_values,
    block_owner,
    block_lengths,
    draft_mask,
    out_weight,
    norm_gain,
    gate_weight,
    up_weight,
):
    devices = lax.axis_size("wide")
    own_index = lax.axis_index("wide")
    head_size = cache_keys.shape[1]
    key_heads = draft_keys.shape[1] // head_size
    group_width = queries.shape[1] // key_heads
    group = group_width // head_size
    sequences = draft_mask.shape[0]
    draft_rows = draft_mask.shape[1]
    all_rows = sequences * draft_rows
    local_rows = queries.shape[0]
    heads_all = key_heads * group
    blocks_per_pair = devices // (sequences * key_heads)
    device_ids = jnp.arange(devices, dtype=jnp.int32)
    owned = (block_owner[None, :] == device_ids[:, None]).astype(jnp.int32)
    device_block = jnp.sum(owned * device_ids[None, :], axis=1)
    device_pair = device_block // blocks_per_pair
    device_sequence = device_pair // key_heads
    device_head = device_pair % key_heads
    device_length = jnp.sum(owned * block_lengths[None, :], axis=1)
    picker = (device_ids == own_index).astype(jnp.int32)
    own_block = jnp.sum(picker * device_block)
    own_sequence = jnp.sum(picker * device_sequence)
    own_head = jnp.sum(picker * device_head)
    own_length = jnp.sum(picker * device_length)
    is_last = own_block % blocks_per_pair == blocks_per_pair - 1
    row_start = own_sequence * draft_rows
    head_numbers = jnp.arange(key_heads, dtype=jnp.int32)
    every_query, every_key, every_value = (
        lax.all_gather(queries, "wide", axis=0, tiled=True),
        lax.all_gather(draft_keys, "wide", axis=0, tiled=True),
        lax.all_gather(draft_values, "wide", axis=0, tiled=True),
    )
    query_columns = own_head * group_width
    key_columns = own_head * head_size
    pair_queries = lax.dynamic_slice_in_dim(
        lax.dynamic_slice_in_dim(every_query, row_start, draft_rows, 0),
        query_columns,
        group_width,
        1,
    )
    pair_keys = lax.dynamic_slice_in_dim(
        lax.dynamic_slice_in_dim(every_key, row_start, draft_rows, 0), key_columns, head_size, 1
    )
    pair_values = lax.dynamic_slice_in_dim(
        lax.dynamic_slice_in_dim(every_value, row_start, draft_rows, 0), key_columns, head_size, 1
    )
    own_head = jnp.sum(picker * device_head)
    query_rows = pair_queries.reshape(draft_rows, group, head_size)
    own_valid = (
        lax.dynamic_index_in_dim(draft_mask, own_sequence, 0, keepdims=False) > 0
    ) & is_last
    running, total, weighted = attend(
        query_rows, cache_keys, cache_values, own_length, pair_keys, pair_values, own_valid
    )
    block_output = (weighted / total[..., None]).astype(jnp.bfloat16)
    slot_peak = lax.dynamic_update_slice(
        jnp.full((all_rows, group), very_low, jnp.float32), running, (row_start, jnp.int32(0))
    ).reshape(devices, local_rows, group)
    slot_total = lax.dynamic_update_slice(
        jnp.zeros((all_rows, group), jnp.float32), total, (row_start, jnp.int32(0))
    ).reshape(devices, local_rows, group)
    slot_output = lax.dynamic_update_slice(
        jnp.zeros((all_rows, group, head_size), jnp.bfloat16),
        block_output,
        (row_start, jnp.int32(0), jnp.int32(0)),
    ).reshape(devices, local_rows, group, head_size)
    back_peak, back_total = (
        lax.all_to_all(slot_peak, "wide", split_axis=0, concat_axis=0, tiled=True),
        lax.all_to_all(slot_total, "wide", split_axis=0, concat_axis=0, tiled=True),
    )
    back_output = lax.all_to_all(slot_output, "wide", split_axis=0, concat_axis=0, tiled=True)
    member = device_head[:, None] == head_numbers[None, :]
    spread = jnp.where(member[:, None, :, None], back_peak[:, :, None, :], very_low)
    highest = jnp.max(spread, axis=0)
    mixing = jnp.exp(spread - highest[None]) * back_total[:, :, None, :]
    row_total = jnp.sum(mixing, axis=0)
    row_weighted = jnp.einsum(
        "srgj,srjc->rgjc", mixing, back_output.astype(jnp.float32), precision=lax.Precision.HIGHEST
    )
    attended_rows = (
        (row_weighted / row_total[..., None])
        .astype(jnp.bfloat16)
        .reshape(local_rows, heads_all * head_size)
    )
    combined = jnp.dot(
        lax.all_gather(attended_rows, "wide", axis=0, tiled=True),
        out_weight,
        preferred_element_type=jnp.float32,
    )
    projected = combined.astype(jnp.bfloat16)
    columns = projected.shape[1]
    branch = lax.optimization_barrier(projected).astype(jnp.float32)
    squares = lax.psum(jnp.sum(branch * branch, axis=1), "wide")
    inverse = lax.rsqrt(squares / (columns * devices) + epsilon)
    gain_part = lax.dynamic_slice_in_dim(norm_gain, own_index * columns, columns, 0)
    normed = (branch * inverse[:, None] * gain_part[None, :]).astype(jnp.bfloat16)
    piece = lax.all_gather(normed, "wide", axis=1, tiled=True)
    gate = jnp.dot(piece, gate_weight, preferred_element_type=jnp.float32)
    upward = jnp.dot(piece, up_weight, preferred_element_type=jnp.float32)
    hidden = (jax.nn.silu(gate) * upward).astype(jnp.bfloat16)
    return (projected, hidden)


def fused_kernel(
    devices,
    owner_ref,
    lengths_ref,
    packed_ref,
    mask_ref,
    gain_ref,
    keys_hbm,
    values_hbm,
    out_hbm,
    gate_hbm,
    up_hbm,
    projected_ref,
    hidden_ref,
    sent,
    gathered,
    query_all,
    keys,
    values,
    outs,
    stats,
    attended,
    branch,
    gate_sum,
    up_sum,
    out_weight,
    gate_weight,
    up_weight,
    local_sem,
    direct_send,
    direct_recv,
    ring_send,
    ring_recv,
):
    me = lax.axis_index("wide")
    depth = devices // 4
    place_z, place_y, place_c = me // 4, lax.rem(me // 2, 2), lax.rem(me, 2)
    mirror_y = me + 2 - 4 * place_y
    mirror_c = me + 1 - 2 * place_c
    head_size = keys.shape[1]
    key_heads = packed_ref.shape[0]
    sequences, draft_rows = mask_ref.shape[0], mask_ref.shape[1]
    senders = devices // sequences
    local_rows = draft_rows // senders
    group = query_all.shape[0] // draft_rows
    blocks_per_pair = devices // (sequences * key_heads)
    capacity = keys.shape[0]

    def block_of(device):
        block = jnp.int32(0)
        for k in range(devices):
            block = block + jnp.where(owner_ref[k] == device, jnp.int32(k), jnp.int32(0))
        return jnp.minimum(block, devices - 1)

    key_copy = pltpu.make_async_copy(keys_hbm, keys, local_sem.at[0])
    value_copy = pltpu.make_async_copy(values_hbm, values, local_sem.at[1])
    key_copy.start()
    value_copy.start()

    barrier = pltpu.get_barrier_semaphore()

    def greet(k, carry):
        pl.semaphore_signal(
            barrier,
            inc=1,
            device_id={"wide": lax.rem(me + k, devices)},
            device_id_type=pl.DeviceIdType.MESH,
        )
        return carry

    lax.fori_loop(1, devices, greet, 0)

    def fill(k, carry):
        target = lax.rem(me + k, devices)
        head = lax.rem(block_of(target) // blocks_per_pair, key_heads)
        sent[target] = packed_ref[head]
        return carry

    lax.fori_loop(1, devices, fill, 0)
    own_block = block_of(me)
    own_pair = own_block // blocks_per_pair
    own_sequence = own_pair // key_heads
    own_head = lax.rem(own_pair, key_heads)
    is_last = jnp.where(
        lax.rem(own_block, blocks_per_pair) == blocks_per_pair - 1, jnp.int32(1), jnp.int32(0)
    )
    own_length = jnp.int32(0)
    for k in range(devices):
        own_length = own_length + jnp.where(owner_ref[k] == me, lengths_ref[k], jnp.int32(0))
    gathered[me] = packed_ref[own_head]
    pl.semaphore_wait(barrier, devices - 1)

    def direct(target, source):
        return pltpu.make_async_remote_copy(
            src_ref=sent.at[target],
            dst_ref=gathered.at[source],
            send_sem=direct_send.at[target],
            recv_sem=direct_recv.at[source],
            device_id={"wide": target},
            device_id_type=pl.DeviceIdType.MESH,
        )

    def send_direct(k, carry):
        direct(lax.rem(me + k, devices), me).start()
        return carry

    lax.fori_loop(1, devices, send_direct, 0)

    weight_copies = []
    for number, (source, target) in enumerate(
        ((out_hbm, out_weight), (gate_hbm, gate_weight), (up_hbm, up_weight))
    ):
        part = source.shape[0] // weight_parts
        for piece in range(weight_parts):
            rows = pl.ds(piece * part, part)
            weight_copies.append(
                pltpu.make_async_copy(
                    source.at[rows],
                    target.at[rows],
                    local_sem.at[2 + number * weight_parts + piece],
                )
            )
    for copy in weight_copies:
        copy.start()

    def wait_direct(k, carry):
        other = lax.rem(me + k, devices)
        descriptor = direct(other, other)
        descriptor.wait_send()
        descriptor.wait_recv()
        return carry

    lax.fori_loop(1, devices, wait_direct, 0)

    def hop(item, direction, source, target):
        buffer, phase = item
        return pltpu.make_async_remote_copy(
            src_ref=buffer.at[source],
            dst_ref=buffer.at[source],
            send_sem=ring_send.at[phase, direction, source],
            recv_sem=ring_recv.at[phase, source],
            device_id={"wide": target},
            device_id_type=pl.DeviceIdType.MESH,
        )

    def launch(items, upward, downward, source, begin):
        for item in items:
            for use, step, direction in ((upward, 4, 0), (downward, -4, 1)):
                if use:

                    @pl.when((place_z + step // 4 >= 0) & (place_z + step // 4 < depth))
                    def _(item=item, step=step, direction=direction):
                        copy = hop(item, direction, source, me + step)
                        copy.start() if begin else copy.wait_send()

            copy = hop(item, 2, source, mirror_y)
            copy.start() if begin else copy.wait_send()
            copy = hop(item, 3, source, mirror_c)
            copy.start() if begin else copy.wait_send()

    def own_send(items, begin=True):
        launch(items, True, True, me, begin)

    def z_step(items, distance, begin=True):
        @pl.when(place_z >= distance)
        def _():
            source = me - 4 * distance
            if begin:
                for item in items:
                    hop(item, 0, source, me).wait_recv()
            launch(items, True, False, source, begin)

        @pl.when(place_z + distance < depth)
        def _():
            source = me + 4 * distance
            if begin:
                for item in items:
                    hop(item, 1, source, me).wait_recv()
            launch(items, False, True, source, begin)

    def y_one(items, source, begin):
        for item in items:
            if begin:
                hop(item, 2, source, me).wait_recv()
            copy = hop(item, 3, source, mirror_c)
            copy.start() if begin else copy.wait_send()

    def y_step(items, distance, begin=True):
        if distance == 0:
            y_one(items, mirror_y, begin)
        else:

            @pl.when(place_z >= distance)
            def _():
                y_one(items, mirror_y - 4 * distance, begin)

            @pl.when(place_z + distance < depth)
            def _():
                y_one(items, mirror_y + 4 * distance, begin)

    def core_wait(items):
        for half in range(devices // 2):
            source = 2 * half + 1 - place_c
            for item in items:
                hop(item, 3, source, me).wait_recv()

    def finish_sends(items):
        own_send(items, False)
        for distance in range(1, depth):
            z_step(items, distance, False)
        for distance in range(depth):
            y_step(items, distance, False)

    pieces = [
        gathered[own_sequence * senders + number].astype(jnp.float32) for number in range(senders)
    ]

    def assembled(begin):
        return jnp.concatenate(
            [piece[begin : begin + local_rows] for piece in pieces], axis=0
        ).astype(jnp.bfloat16)

    for j in range(group):
        query_all[j * draft_rows : (j + 1) * draft_rows] = assembled(j * local_rows)
    draft_keys = assembled(group * local_rows)
    draft_values = assembled((group + 1) * local_rows)
    own_mask = mask_ref[own_sequence] * is_last

    tile_heads = group // tiles
    tile_rows = tile_heads * draft_rows
    unit = math.log2(math.e) / math.sqrt(head_size)
    steps = capacity // chunk_rows
    lanes = lax.broadcasted_iota(jnp.int32, (draft_rows, stats.shape[2]), 1)
    key_copy.wait()
    value_copy.wait()

    def update(state, scores, block_values):
        peak, total, weighted = state
        newest = jnp.maximum(peak, jnp.max(scores, axis=1, keepdims=True))
        factor = jnp.exp2(peak - newest)
        weights = jnp.exp2(scores - newest)
        total = total * factor + jnp.sum(weights, axis=1, keepdims=True)
        weighted = weighted * factor + jnp.dot(
            weights.astype(jnp.bfloat16), block_values, preferred_element_type=jnp.float32
        )
        return newest, total, weighted

    own_stats = jnp.zeros((draft_rows, stats.shape[2]), jnp.float32)
    for tile in range(tiles):
        query = query_all[tile * tile_rows : (tile + 1) * tile_rows]

        def advance(number, state, query=query):
            begin = pl.multiple_of(number * chunk_rows, chunk_rows)
            scores = lax.dot_general(
                query,
                keys[pl.ds(begin, chunk_rows)],
                (((1,), (1,)), ((), ())),
                preferred_element_type=jnp.float32,
            )
            position = begin + lax.broadcasted_iota(jnp.int32, (1, chunk_rows), 1)
            bias = jnp.where(position < own_length, 0.0, very_low)
            return update(state, scores * unit + bias, values[pl.ds(begin, chunk_rows)])

        state = (
            jnp.full((tile_rows, 1), very_low, jnp.float32),
            jnp.zeros((tile_rows, 1), jnp.float32),
            jnp.zeros((tile_rows, head_size), jnp.float32),
        )
        cuts = [steps * cut // depth for cut in range(depth + 1)]
        for cut in range(depth):
            state = lax.fori_loop(cuts[cut], cuts[cut + 1], advance, state)
            if tile > 0 and cut == depth // 2:
                z_step([(outs.at[tile - 1], tile - 1)], 1)
        scores = lax.dot_general(
            query, draft_keys, (((1,), (1,)), ((), ())), preferred_element_type=jnp.float32
        )
        visible = jnp.concatenate([own_mask] * tile_heads, axis=0) > 0
        peak, total, weighted = update(
            state, jnp.where(visible, scores * unit, very_low), draft_values
        )
        outs[tile, me] = (weighted / total).astype(jnp.bfloat16)
        for k in range(tile_heads):
            head = tile * tile_heads + k
            rows = slice(k * draft_rows, (k + 1) * draft_rows)
            own_stats = jnp.where(lanes == head, peak[rows], own_stats)
            own_stats = jnp.where(lanes == group + head, total[rows], own_stats)
        if tile + 1 == tiles:
            stats[me] = own_stats
            last = [(outs.at[tile], tile), (stats, tiles)]
            own_send(last)
        else:
            own_send([(outs.at[tile], tile)])

    first = [(outs.at[tile], tile) for tile in range(tiles - 1)]
    for distance in range(1, depth):
        if distance + 1 < depth:
            z_step(first, distance + 1)
        y_step(first, distance - 1)
        z_step(last, distance)
        y_step(last, distance - 1)
    y_step(first, depth - 1)
    y_step(last, depth - 1)
    core_wait([(outs.at[tile], tile) for tile in range(tiles)] + [(stats, tiles)])

    for pair in range(sequences * key_heads):
        owners = [owner_ref[pair * blocks_per_pair + b] for b in range(blocks_per_pair)]
        each = [stats[owner] for owner in owners]
        highest = functools.reduce(jnp.maximum, each)
        mixing = [
            jnp.exp2(one - highest) * pltpu.roll(one, one.shape[1] - group, 1) for one in each
        ]
        mixing_sum = functools.reduce(jnp.add, mixing)
        shares = [one / mixing_sum for one in mixing]
        top = pair // key_heads * draft_rows
        for tile in range(tiles):
            held = [outs[tile, owner].astype(jnp.float32) for owner in owners]
            for k in range(tile_heads):
                head = tile * tile_heads + k
                rows = slice(k * draft_rows, (k + 1) * draft_rows)
                mixed = functools.reduce(
                    jnp.add,
                    [share[:, head : head + 1] * one[rows] for share, one in zip(shares, held)],
                )
                left = (pair % key_heads * group + head) * head_size
                attended[top : top + draft_rows, left : left + head_size] = mixed.astype(
                    jnp.bfloat16
                )

    for copy in weight_copies[:weight_parts]:
        copy.wait()
    projected = jnp.dot(
        attended[...], out_weight[...], preferred_element_type=jnp.float32
    ).astype(jnp.bfloat16)
    branch[me] = projected
    phase = [(branch, tiles + 1)]
    own_send(phase)
    projected_ref[...] = projected
    for copy in weight_copies[weight_parts:]:
        copy.wait()

    columns = branch.shape[2]
    gate_sum[...] = jnp.zeros_like(gate_sum)
    up_sum[...] = jnp.zeros_like(up_sum)

    def absorb(source, squares):
        part = branch[source].astype(jnp.float32)
        scaled = (part * gain_ref[source]).astype(jnp.bfloat16)
        rows = pl.ds(pl.multiple_of(source * columns, columns), columns)
        gate_sum[...] += jnp.dot(scaled, gate_weight[rows], preferred_element_type=jnp.float32)
        up_sum[...] += jnp.dot(scaled, up_weight[rows], preferred_element_type=jnp.float32)
        return squares + jnp.sum(part * part, axis=1, keepdims=True)

    squares = absorb(me, jnp.zeros((branch.shape[1], 1), jnp.float32))
    z_step(phase, 1)
    y_step(phase, 0)
    squares = absorb(mirror_y, squares)
    for distance in range(2, depth):
        z_step(phase, distance)
        y_step(phase, distance - 1)

    def own_plane(row):
        def body(k, total):
            return absorb(4 * lax.rem(place_z + k, depth) + 2 * row + place_c, total)

        return body

    def other_plane(row):
        def body(k, total):
            source = 4 * lax.rem(place_z + k, depth) + 2 * row + 1 - place_c
            hop(phase[0], 3, source, me).wait_recv()
            return absorb(source, total)

        return body

    squares = lax.fori_loop(1, depth, own_plane(place_y), squares)
    squares = lax.fori_loop(0, depth, other_plane(place_y), squares)
    y_step(phase, depth - 1)
    squares = lax.fori_loop(1, depth, own_plane(1 - place_y), squares)
    squares = lax.fori_loop(0, depth, other_plane(1 - place_y), squares)
    inverse = lax.rsqrt(squares / (columns * devices) + epsilon)
    gate = gate_sum[...] * inverse
    hidden_ref[...] = (gate / (1.0 + jnp.exp(-gate)) * (up_sum[...] * inverse)).astype(
        jnp.bfloat16
    )
    finish_sends([(outs.at[tile], tile) for tile in range(tiles)] + [(stats, tiles)] + phase)


def fused_device(
    queries,
    draft_keys,
    draft_values,
    cache_keys,
    cache_values,
    block_owner,
    block_lengths,
    draft_mask,
    out_weight,
    norm_gain,
    gate_weight,
    up_weight,
):
    devices = lax.axis_size("wide")
    capacity, head_size = cache_keys.shape
    key_heads = draft_keys.shape[1] // head_size
    group = queries.shape[1] // head_size // key_heads
    local_rows = queries.shape[0]
    sequences, draft_rows = draft_mask.shape[:2]
    rows = sequences * draft_rows
    columns, units = out_weight.shape[1], gate_weight.shape[1]

    def by_head(array, count):
        parted = array.reshape(local_rows, key_heads, count, head_size)
        return parted.transpose(1, 2, 0, 3).reshape(key_heads, count * local_rows, head_size)

    packed = jnp.concatenate(
        [by_head(queries, group), by_head(draft_keys, 1), by_head(draft_values, 1)], axis=1
    )
    vmem = pl.BlockSpec(memory_space=pltpu.VMEM)
    smem = pl.BlockSpec(memory_space=pltpu.SMEM)
    hbm = pl.BlockSpec(memory_space=pl.ANY)
    half = jnp.bfloat16
    return pl.pallas_call(
        functools.partial(fused_kernel, devices),
        out_shape=(
            jax.ShapeDtypeStruct((rows, columns), half),
            jax.ShapeDtypeStruct((rows, units), half),
        ),
        in_specs=[smem, smem, vmem, vmem, vmem, hbm, hbm, hbm, hbm, hbm],
        out_specs=(vmem, vmem),
        scratch_shapes=[
            pltpu.VMEM((devices,) + packed.shape[1:], half),
            pltpu.VMEM((devices,) + packed.shape[1:], half),
            pltpu.VMEM((group * draft_rows, head_size), half),
            pltpu.VMEM((capacity, head_size), half),
            pltpu.VMEM((capacity, head_size), half),
            pltpu.VMEM((tiles, devices, group // tiles * draft_rows, head_size), half),
            pltpu.VMEM((devices, draft_rows, head_size), jnp.float32),
            pltpu.VMEM((rows, out_weight.shape[0]), half),
            pltpu.VMEM((devices, rows, columns), half),
            pltpu.VMEM((rows, units), jnp.float32),
            pltpu.VMEM((rows, units), jnp.float32),
            pltpu.VMEM(out_weight.shape, half),
            pltpu.VMEM(gate_weight.shape, half),
            pltpu.VMEM(up_weight.shape, half),
            pltpu.SemaphoreType.DMA((2 + 3 * weight_parts,)),
            pltpu.SemaphoreType.DMA((devices,)),
            pltpu.SemaphoreType.DMA((devices,)),
            pltpu.SemaphoreType.DMA((tiles + 2, 4, devices)),
            pltpu.SemaphoreType.DMA((tiles + 2, devices)),
        ],
        compiler_params=pltpu.CompilerParams(
            collective_id=0, has_side_effects=True, vmem_limit_bytes=62 * 1024 * 1024
        ),
    )(
        block_owner,
        block_lengths,
        packed,
        draft_mask,
        norm_gain.reshape(devices, 1, columns),
        cache_keys,
        cache_values,
        out_weight,
        gate_weight,
        up_weight,
    )


def per_device(*arrays):
    queries, cache_keys, draft_mask = arrays[0], arrays[3], arrays[7]
    out_weight, gate_weight = arrays[8], arrays[10]
    head_size = cache_keys.shape[1]
    key_heads = arrays[1].shape[1] // head_size
    group = queries.shape[1] // head_size // key_heads
    whole_tiles = (
        queries.shape[0] % 8 == 0
        and lax.axis_size("wide") % 4 == 0
        and draft_mask.shape[1] % 8 == 0
        and head_size % 128 == 0
        and 2 * group <= head_size
        and group % tiles == 0
        and out_weight.shape[1] % 128 == 0
        and gate_weight.shape[1] % 128 == 0
        and cache_keys.shape[0] % chunk_rows == 0
        and out_weight.shape[0] % (16 * weight_parts) == 0
        and gate_weight.shape[0] % (16 * weight_parts) == 0
    )
    return fused_device(*arrays) if whole_tiles else plain_device(*arrays)


def solution(mesh):
    placed = (
        P(("grp", "wide"), None),
        P(("grp", "wide"), None),
        P(("grp", "wide"), None),
        P(("grp", "wide"), None),
        P(("grp", "wide"), None),
        P("grp"),
        P("grp"),
        P("grp", None, None),
        P(None, "wide"),
        P(),
        P(None, "wide"),
        P(None, "wide"),
    )
    return jax.shard_map(
        per_device,
        mesh=mesh,
        in_specs=placed,
        out_specs=(P("grp", "wide"), P("grp", "wide")),
        check_vma=False,
    )
```
